128 devices in a mesh: pipe: 8 (over y, core), tensor: 16 (over x, z).
Axes of the slice: x: 4, y: 4, z: 4, core: 2. Of those that a mesh axis runs over, the one named last changes fastest.
Arguments:
- inputs: bfloat16 [128, 4096], P(None, 'tensor'), may hold values from -6 to 6
- out_grad: bfloat16 [128, 4096], P(None, 'tensor'), may hold values from -6 to 6
- norm_gain: float32 [8, 4096], P('pipe'), may hold values from 0.25 to 1.75
- gate_weight: bfloat16 [8, 4096, 14336], P('pipe', None, 'tensor'), may hold values from -0.125 to 0.125
- up_weight: bfloat16 [8, 4096, 14336], P('pipe', None, 'tensor'), may hold values from -0.125 to 0.125
- down_weight: bfloat16 [8, 14336, 4096], P('pipe', 'tensor'), may hold values from -0.0625 to 0.0625
- block_mask: int32 [8, 3, 32, 112], P('pipe', None, None, 'tensor'), may hold values from 0 to 1, as said below
Outputs:
- section_out: float32 [8, 128, 4096], P('pipe')
- section_grad: float32 [8, 128, 4096], P('pipe')
The draws below stay inside these ranges and needn't reach their ends.
Inputs may be any that keep to these rules, and one draw needn't show every extreme that they name: `block_mask`: 1 keeps a block, 0 drops it; the share kept differs from one block column to another.
All inputs are finite; a program needn't handle non-finite values.
Results may differ from the reference program's by a relative error of at most 0.02.
Values may be sent and summed in bfloat16 or wider, within the bound.
A program may use at most 128 MiB of HBM per device.

```python
import jax
import jax.numpy as jnp
from jax import lax

D = 4096
FF = 14336
BLOCK = 128
ROWS = 64
MB = 2
LAYERS = 8


def draw_block_mask(key, part):
    first, second = jax.random.split(jax.random.fold_in(key, 7))
    shape = (LAYERS, 3, D // BLOCK, FF // BLOCK)
    levels = jax.random.randint(first, (LAYERS, 3, 1, FF // BLOCK), 20, 81)
    draws = jax.random.randint(second, shape, 0, 100)
    return (draws < levels).astype(jnp.int32)


def shard_levels(own_key, shape, shards, low, high):
    level, own = 1.0, jax.random.fold_in(own_key, 6)
    for dim, shards_of in shards:
        steps = jnp.exp(jax.random.uniform(jax.random.fold_in(own, dim), (shards_of,), jnp.float32, low / len(shards), high / len(shards)))
        level = level * jnp.repeat(steps, shape[dim] // shards_of).reshape([-1 if axis == dim else 1 for axis in range(len(shape))])
    return level


def noise(own_key, shape, deviation, reach, pieces=(), kind=jnp.bfloat16):
    level = shard_levels(own_key, shape, pieces, -0.22, 0.18) if pieces else 1.0
    array = jax.random.normal(own_key, shape, jnp.float32) * deviation * level
    return jnp.minimum(jnp.maximum(array, -reach), reach).astype(kind)


def setup_inputs(seed: int = 0) -> dict:
    seeds = jax.random.split(jax.random.key(seed), 8)
    inputs = noise(seeds[0], (MB * ROWS, D), 1.0, 6.0, ((1, 16),))
    out_grad = noise(seeds[1], (MB * ROWS, D), 1.0, 6.0, ((1, 16),))
    norm_gain = jnp.clip(1.0 + 0.15 * jax.random.normal(seeds[2], (LAYERS, D), jnp.float32), 0.25, 1.75)
    gate_weight = noise(seeds[3], (LAYERS, D, FF), (D // 2) ** -0.5, 0.125, ((0, 8), (2, 16)))
    up_weight = noise(seeds[4], (LAYERS, D, FF), (D // 2) ** -0.5, 0.125, ((0, 8), (2, 16)))
    down_weight = noise(seeds[5], (LAYERS, FF, D), (FF // 2) ** -0.5, 0.0625, ((0, 8), (1, 16)))
    block_mask = draw_block_mask(jax.random.fold_in(seeds[7], 71), 0)
    return {"inputs": inputs, "out_grad": out_grad, "norm_gain": norm_gain, "gate_weight": gate_weight, "up_weight": up_weight, "down_weight": down_weight, "block_mask": block_mask}


def masked_blocks(weight, mask):
    rows, cols = weight.shape
    shaped = weight.reshape(rows // BLOCK, BLOCK, cols // BLOCK, BLOCK)
    return (shaped * mask.astype(weight.dtype)[:, None, :, None]).reshape(rows, cols)

def reference(inputs, out_grad, norm_gain, gate_weight, up_weight, down_weight, block_mask):
    eps = 1e-05
    state = inputs.astype(jnp.float32)
    saved = []
    outs_list = []
    for layer in range(LAYERS):
        gmat = masked_blocks(gate_weight[layer], block_mask[layer, 0])
        umat = masked_blocks(up_weight[layer], block_mask[layer, 1])
        dmat = masked_blocks(down_weight[layer], block_mask[layer, 2].T)
        xval = state
        scale = lax.rsqrt(lax.optimization_barrier(jnp.mean(xval * xval, axis=-1, keepdims=True)) + eps)
        normed = (xval * scale * norm_gain[layer]).astype(jnp.bfloat16)
        gate_matrix = jnp.dot(normed, gmat, preferred_element_type=jnp.float32)
        upval = jnp.dot(normed, umat, preferred_element_type=jnp.float32)
        hidden = (jax.nn.silu(gate_matrix) * upval).astype(jnp.bfloat16)
        branch = jnp.dot(hidden, dmat, preferred_element_type=jnp.float32)
        state = xval + branch
        outs_list.append(state)
        saved.append((xval, scale, gate_matrix, upval))
    grads_list = [None] * LAYERS
    cot = out_grad.astype(jnp.float32)
    for layer in range(LAYERS - 1, -1, -1):
        gmat = masked_blocks(gate_weight[layer], block_mask[layer, 0])
        umat = masked_blocks(up_weight[layer], block_mask[layer, 1])
        dmat = masked_blocks(down_weight[layer], block_mask[layer, 2].T)
        xval, scale, gate_matrix, upval = saved[layer]
        cot_low = cot.astype(jnp.bfloat16)
        dhid = jnp.dot(cot_low, dmat.T, preferred_element_type=jnp.float32)
        sig = jax.nn.sigmoid(gate_matrix)
        dgate = (dhid * upval * sig * (1.0 + gate_matrix * (1.0 - sig))).astype(jnp.bfloat16)
        dup = (dhid * gate_matrix * sig).astype(jnp.bfloat16)
        dnorm = jnp.dot(dgate, gmat.T, preferred_element_type=jnp.float32) + jnp.dot(dup, umat.T, preferred_element_type=jnp.float32)
        avec = dnorm * norm_gain[layer]
        inner = lax.optimization_barrier(jnp.mean(avec * xval, axis=-1, keepdims=True))
        back = scale * avec - xval * scale * scale * scale * inner
        cot = cot + back
        grads_list[layer] = cot
    return (jnp.stack(outs_list), jnp.stack(grads_list))
```

```python
import functools

import jax
import jax.numpy as jnp
from jax import lax
from jax.experimental import pallas as pl
from jax.experimental.pallas import tpu as pltpu
from jax.sharding import PartitionSpec as P

EPS = 1e-05
MB = 2
CHUNK = 256
BLOCK = 128
F32 = jnp.float32
BF16 = jnp.bfloat16
MESH = pl.DeviceIdType.MESH

STEP = (2, 1, 3, 0)
OFFSETS = [(a, b) for a in STEP for b in STEP]
NEGATED = [OFFSETS.index(((-a) % 4, (-b) % 4)) for a, b in OFFSETS]


def hops(k):
    return sum(min(d, 4 - d) for d in OFFSETS[k])


FAR_FIRST = sorted(range(16), key=lambda k: -hops(k))
SELF = 15


def step_of(u):
    return lax.rem(2 + 3 * u + 3 * (u * (u - 1) // 2), 4)


def kernel(
    x_ref, g_ref, gain_ref, mask_ref, gate_hbm, up_hbm, down_hbm,
    outf_hbm, outb_hbm,
    wgu, wd, wgu_t, wd_t, xin, cin, recv_f, recv_b, send_f, send_b, hsend, csend,
    ret_f, ret_b, pre, rows, xg, dgu, gain_in, gain_out,
    load_sem, xin_sem, cin_sem, rsf_sem, rsb_sem, retf_sem, retb_sem, send_sem, out_sem,
):
    me = lax.axis_index("pipe")
    my = lax.axis_index("tensor")
    my_a, my_b = my // 4, lax.rem(my, 4)
    rows_of = xin.shape[1]
    width = xin.shape[2]
    hidden = wd.shape[0]
    blocks = hidden // BLOCK
    last = 7

    def to(k):
        a, b = OFFSETS[k]
        return lax.rem(my_a + a, 4) * 4 + lax.rem(my_b + b, 4)

    def source(k):
        a, b = OFFSETS[k]
        return lax.rem(my_a + (4 - a), 4) * 4 + lax.rem(my_b + (4 - b), 4)

    def cols(k):
        return pl.ds(k * CHUNK, CHUNK)

    def lanes(c):
        return pl.ds(pl.multiple_of(c * CHUNK, CHUNK), CHUNK)

    def remote(src, dst, sent, got, stage, index):
        return pltpu.make_async_remote_copy(
            src_ref=src, dst_ref=dst, send_sem=sent, recv_sem=got,
            device_id=(stage, index), device_id_type=MESH,
        )

    loads = []
    for k in range(16):
        rows_hbm = lanes(source(k))
        loads.append(pltpu.make_async_copy(
            gate_hbm.at[0, rows_hbm, :], wgu.at[pl.ds(k * CHUNK, CHUNK), pl.ds(0, hidden)], load_sem.at[0, k]))
        loads.append(pltpu.make_async_copy(
            up_hbm.at[0, rows_hbm, :], wgu.at[pl.ds(k * CHUNK, CHUNK), pl.ds(hidden, hidden)], load_sem.at[1, k]))
    for k in range(16):
        loads.append(pltpu.make_async_copy(
            down_hbm.at[0, :, lanes(to(k))], wd.at[:, cols(k)], load_sem.at[2, k]))
    for copy in loads:
        copy.start()

    barrier = pltpu.get_barrier_semaphore()
    for k in range(15):
        pl.semaphore_signal(barrier, inc=1, device_id=(me, to(k)), device_id_type=MESH)

    @pl.when(me > 0)
    def _():
        for k in range(16):
            pl.semaphore_signal(barrier, inc=1, device_id=(me - 1, to(k)), device_id_type=MESH)

    @pl.when(me < last)
    def _():
        for k in range(16):
            pl.semaphore_signal(barrier, inc=1, device_id=(me + 1, to(k)), device_id_type=MESH)

    edge = (me == 0) | (me == last)

    @pl.when(edge)
    def _():
        pl.semaphore_wait(barrier, 31)

    @pl.when(jnp.logical_not(edge))
    def _():
        pl.semaphore_wait(barrier, 47)

    def gather(src_ref, dst, got, sent):
        for m in range(MB):
            src = src_ref.at[pl.ds(m * rows_of, rows_of), :]
            pltpu.make_async_copy(src, dst.at[m, :, cols(SELF)], got.at[m]).start()
            for k in FAR_FIRST[:15]:
                remote(src, dst.at[m, :, cols(k)], sent.at[m], got.at[m], me, to(k)).start()

    @pl.when(me == 0)
    def _():
        gather(x_ref, xin, xin_sem, send_sem.at[4])

    @pl.when(me == last)
    def _():
        gather(g_ref, cin, cin_sem, send_sem.at[4])

    for k in range(16):
        gain_in[:, k * CHUNK:(k + 1) * CHUNK] = gain_ref[:, lanes(source(k))]
        gain_out[:, k * CHUNK:(k + 1) * CHUNK] = gain_ref[:, lanes(to(k))]

    def keep(which, i, j):
        return jnp.full((BLOCK, BLOCK), mask_ref[0, which, i, j].astype(F32)).astype(BF16)

    @pl.loop(0, 16)
    def _(k):
        a, b = step_of(k // 4), step_of(lax.rem(k, 4))
        c = lax.rem(my_a + 4 - a, 4) * 4 + lax.rem(my_b + 4 - b, 4)
        at = pl.ds(pl.multiple_of(k * CHUNK, CHUNK), CHUNK)
        for which in range(2):
            piece = wgu.at[at, pl.ds(which * hidden, hidden)]
            pltpu.make_async_copy(piece, piece, load_sem.at[which, k]).wait()
        for half in range(2):
            r = pl.ds(pl.multiple_of(k * CHUNK + half * BLOCK, BLOCK), BLOCK)
            for which in range(2):
                for j in range(blocks):
                    o = which * hidden + j * BLOCK
                    wgu[r, o:o + BLOCK] = wgu[r, o:o + BLOCK] * keep(which, c * 2 + half, j)

    @pl.loop(0, 16)
    def _(k):
        a, b = step_of(k // 4), step_of(lax.rem(k, 4))
        c = lax.rem(my_a + a, 4) * 4 + lax.rem(my_b + b, 4)
        piece = wd.at[:, pl.ds(pl.multiple_of(k * CHUNK, CHUNK), CHUNK)]
        pltpu.make_async_copy(piece, piece, load_sem.at[2, k]).wait()
        for half in range(2):
            r = pl.ds(pl.multiple_of(k * CHUNK + half * BLOCK, BLOCK), BLOCK)
            for j in range(blocks):
                o = j * BLOCK
                wd[o:o + BLOCK, r] = wd[o:o + BLOCK, r] * keep(2, c * 2 + half, j)

    def transpose_weights():
        @pl.loop(0, 16)
        def _(k):
            u, v = k // 4, lax.rem(k, 4)
            nu, nv = lax.rem(u * 2, 3) + 3 * (u // 3), lax.rem(v * 2, 3) + 3 * (v // 3)
            n = nu * 4 + nv
            here = pl.ds(pl.multiple_of(k * CHUNK, CHUNK), CHUNK)
            there = pl.ds(pl.multiple_of(n * CHUNK, CHUNK), CHUNK)
            for j in range(2 * hidden // CHUNK):
                o = j * CHUNK
                wgu_t[o:o + CHUNK, there] = wgu[here, o:o + CHUNK].T
            for j in range(blocks):
                o = j * BLOCK
                wd_t[there, o:o + BLOCK] = wd[o:o + BLOCK, here].T

    @pl.when(me >= 4)
    def _():
        transpose_weights()

    def whole(ref, sem):
        pltpu.make_async_copy(ref, ref, sem).wait()

    def forward_compute(m):
        whole(xin.at[m], xin_sem.at[m])

        @pl.when(me > 0)
        def _():
            remote(xin.at[m], ret_f.at[m], send_sem.at[5, m], retf_sem.at[m], me - 1, my).start()

        square = jnp.zeros((rows_of, 1), F32)
        for k in range(16):
            part = xin[m, :, k * CHUNK:(k + 1) * CHUNK].astype(F32)
            square = square + jnp.sum(part * part, axis=1, keepdims=True)
            xg[:, k * CHUNK:(k + 1) * CHUNK] = (part * gain_in[:, k * CHUNK:(k + 1) * CHUNK]).astype(BF16)
        scale = lax.rsqrt(square * (1.0 / width) + EPS)
        rows[m] = jnp.broadcast_to(scale, (rows_of, BLOCK))
        both = jnp.dot(xg[...], wgu[...], preferred_element_type=F32) * scale
        pre[m] = both
        gate, up = both[:, :hidden], both[:, hidden:]
        act = (gate * jax.nn.sigmoid(gate) * up).astype(BF16)
        for n in range(2):
            o = n * 8 * CHUNK
            part = jnp.dot(act, wd[:, o:o + 8 * CHUNK], preferred_element_type=F32)
            for q in range(8):
                send_f[m, n * 8 + q] = part[:, q * CHUNK:(q + 1) * CHUNK].astype(BF16)
            for q in range(8):
                k = n * 8 + q
                if k != SELF:
                    remote(send_f.at[m, k], recv_f.at[m, k], send_sem.at[0, m], rsf_sem.at[m], me, to(k)).start()

    def total(recv, send, m, sem):
        whole(recv.at[m, pl.ds(0, 15)], sem.at[m])
        acc = send[m, SELF].astype(F32)
        for k in range(15):
            acc = acc + recv[m, k].astype(F32)
        return acc

    own = slice(SELF * CHUNK, (SELF + 1) * CHUNK)

    def forward_reduce(m):
        acc = total(recv_f, send_f, m, rsf_sem)
        hsend[m] = (xin[m, :, own].astype(F32) + acc).astype(BF16)

        @pl.when(me < last)
        def _():
            for k in FAR_FIRST:
                remote(hsend.at[m], xin.at[m, :, cols(k)], send_sem.at[1, m], xin_sem.at[m], me + 1, to(k)).start()

        @pl.when(me == last)
        def _():
            ret_f[m, :, own] = hsend[m]
            for k in FAR_FIRST[:15]:
                remote(hsend.at[m], ret_f.at[m, :, cols(k)], send_sem.at[1, m], retf_sem.at[m], me, to(k)).start()

    def backward_compute(m):
        whole(cin.at[m], cin_sem.at[m])

        @pl.when(me < last)
        def _():
            remote(cin.at[m], ret_b.at[m], send_sem.at[6, m], retb_sem.at[m], me + 1, my).start()

        dh = jnp.dot(cin[m], wd_t[...], preferred_element_type=F32)
        gate, up = pre[m, :, :hidden], pre[m, :, hidden:]
        sig = jax.nn.sigmoid(gate)
        dgate = (dh * up * sig * (1.0 + gate * (1.0 - sig))).astype(BF16)
        dup = (dh * gate * sig).astype(BF16)
        dgu[:, :hidden] = dgate
        dgu[:, hidden:] = dup
        inner = jnp.sum(dgate.astype(F32) * gate + dup.astype(F32) * up, axis=1, keepdims=True)
        scale = rows[m, :, 0:1]
        inner = inner * scale * scale * (1.0 / width)
        for n in range(4):
            o = n * 4 * CHUNK
            part = jnp.dot(dgu[...], wgu_t[:, o:o + 4 * CHUNK], preferred_element_type=F32)
            for q in range(4):
                k = n * 4 + q
                s = NEGATED[k]
                xval = xin[m, :, s * CHUNK:(s + 1) * CHUNK].astype(F32)
                back = part[:, q * CHUNK:(q + 1) * CHUNK] * gain_out[:, k * CHUNK:(k + 1) * CHUNK] * scale
                send_b[m, k] = (back - xval * inner).astype(BF16)
            for q in range(4):
                k = n * 4 + q
                if k != SELF:
                    remote(send_b.at[m, k], recv_b.at[m, k], send_sem.at[2, m], rsb_sem.at[m], me, to(k)).start()

    def backward_reduce(m):
        acc = total(recv_b, send_b, m, rsb_sem)
        csend[m] = (cin[m, :, own].astype(F32) + acc).astype(BF16)

        @pl.when(me > 0)
        def _():
            for k in FAR_FIRST:
                remote(csend.at[m], cin.at[m, :, cols(k)], send_sem.at[3, m], cin_sem.at[m], me - 1, to(k)).start()

        @pl.when(me == 0)
        def _():
            ret_b[m, :, own] = csend[m]
            for k in FAR_FIRST[:15]:
                remote(csend.at[m], ret_b.at[m, :, cols(k)], send_sem.at[3, m], retb_sem.at[m], me, to(k)).start()

    @pl.loop(0, MB + 1)
    def _(i):
        @pl.when(i < MB)
        def _():
            forward_compute(i)

        @pl.when((i > 0) & (me < last))
        def _():
            forward_reduce(i - 1)

    @pl.when(me < 4)
    def _():
        transpose_weights()

    @pl.loop(0, MB + 1)
    def _(i):
        @pl.when(i < MB)
        def _():
            backward_compute(i)

        @pl.when((i > 0) & (me == last))
        def _():
            forward_reduce(i - 1)

        @pl.when(i > 0)
        def _():
            backward_reduce(i - 1)

    def put(ret, sem, out_hbm, which, edge):
        @pl.loop(0, MB)
        def _(m):
            @pl.when(me == edge)
            def _():
                whole(ret.at[m, :, pl.ds(0, 15 * CHUNK)], sem.at[m])

            @pl.when(me != edge)
            def _():
                whole(ret.at[m], sem.at[m])

            for k in range(16):
                pltpu.make_async_copy(
                    ret.at[m, :, cols(k)],
                    out_hbm.at[0, pl.ds(pl.multiple_of(m * rows_of, 16), rows_of), lanes(source(k))],
                    out_sem.at[which, m],
                ).start()

    put(ret_f, retf_sem, outf_hbm, 0, last)
    put(ret_b, retb_sem, outb_hbm, 1, 0)

    @pl.loop(0, MB)
    def _(m):
        fifteen = recv_f.at[m, pl.ds(0, 15)]
        whole(fifteen, send_sem.at[0, m])
        whole(fifteen, send_sem.at[2, m])

        @pl.when(me < last)
        def _():
            whole(xin.at[m], send_sem.at[1, m])
            whole(xin.at[m], send_sem.at[6, m])

        @pl.when(me == last)
        def _():
            whole(fifteen, send_sem.at[1, m])

        @pl.when(me > 0)
        def _():
            whole(xin.at[m], send_sem.at[3, m])
            whole(xin.at[m], send_sem.at[5, m])

        @pl.when(me == 0)
        def _():
            whole(fifteen, send_sem.at[3, m])

        @pl.when((me == 0) | (me == last))
        def _():
            whole(fifteen, send_sem.at[4, m])

        whole(ret_f.at[m], out_sem.at[0, m])
        whole(ret_b.at[m], out_sem.at[1, m])


def local(inputs, out_grad, norm_gain, gate_weight, up_weight, down_weight, block_mask):
    count, chunk = inputs.shape
    width = norm_gain.shape[1]
    hidden = gate_weight.shape[2]
    r = count // MB
    vmem = pl.BlockSpec(memory_space=pltpu.VMEM)
    anyspace = pl.BlockSpec(memory_space=pl.ANY)
    dma = pltpu.SemaphoreType.DMA
    full = lambda dtype=BF16: pltpu.VMEM((MB, r, width), dtype)
    parts = lambda: pltpu.VMEM((MB, 16, r, chunk), BF16)
    forward, backward = pl.pallas_call(
        kernel,
        out_shape=[jax.ShapeDtypeStruct((1, count, width), BF16)] * 2,
        in_specs=[vmem, vmem, vmem, pl.BlockSpec(memory_space=pltpu.SMEM), anyspace, anyspace, anyspace],
        out_specs=[anyspace, anyspace],
        scratch_shapes=[
            pltpu.VMEM((width, 2 * hidden), BF16),
            pltpu.VMEM((hidden, width), BF16),
            pltpu.VMEM((2 * hidden, width), BF16),
            pltpu.VMEM((width, hidden), BF16),
            full(), full(),
            parts(), parts(), parts(), parts(),
            pltpu.VMEM((MB, r, chunk), BF16),
            pltpu.VMEM((MB, r, chunk), BF16),
            full(), full(),
            pltpu.VMEM((MB, r, 2 * hidden), F32),
            pltpu.VMEM((MB, r, BLOCK), F32),
            pltpu.VMEM((r, width), BF16),
            pltpu.VMEM((r, 2 * hidden), BF16),
            pltpu.VMEM((1, width), F32),
            pltpu.VMEM((1, width), F32),
            dma((3, 16)),
            dma((MB,)), dma((MB,)), dma((MB,)), dma((MB,)), dma((MB,)), dma((MB,)),
            dma((7, MB)),
            dma((2, MB)),
        ],
        compiler_params=pltpu.CompilerParams(
            collective_id=0, has_side_effects=True, vmem_limit_bytes=67043328
        ),
        name="window",
    )(inputs, out_grad, norm_gain, block_mask, gate_weight, up_weight, down_weight)
    return forward.astype(F32), backward.astype(F32)


def solution(mesh):
    in_specs = (
        P(None, "tensor"),
        P(None, "tensor"),
        P("pipe", None),
        P("pipe", None, "tensor"),
        P("pipe", None, "tensor"),
        P("pipe", "tensor", None),
        P("pipe", None, None, "tensor"),
    )
    out_specs = (P("pipe", None, None), P("pipe", None, None))
    return jax.shard_map(local, mesh=mesh, in_specs=in_specs, out_specs=out_specs, check_vma=False)
```

```python
import functools

import jax
import jax.numpy as jnp
from jax import lax
from jax.experimental import pallas as pl
from jax.experimental.pallas import tpu as pltpu
from jax.sharding import PartitionSpec as P

EPS = 1e-05
MB = 4
CHUNK = 256
BLOCK = 128
F32 = jnp.float32
BF16 = jnp.bfloat16
MESH = pl.DeviceIdType.MESH

OFFSETS = [
    (2, 2),
    (2, 1), (2, 3), (1, 2), (3, 2),
    (2, 0), (0, 2), (1, 1), (3, 3), (1, 3), (3, 1),
    (1, 0), (3, 0), (0, 1), (0, 3),
    (0, 0),
]
NEGATED = [OFFSETS.index(((-a) % 4, (-b) % 4)) for a, b in OFFSETS]
GROUPS = ((11, 16), (5, 11), (0, 5))
FORWARD_AT = -1
BACKWARD_AT = -1
GROUP_OF = [next(g for g, (lo, hi) in enumerate(GROUPS) if lo <= k < hi) for k in range(16)]


def packed(values):
    word = sum(v << (2 * k) for k, v in enumerate(values))
    return word - (1 << 32) if word >= 1 << 31 else word


PACKED = (packed([a for a, b in OFFSETS]), packed([b for a, b in OFFSETS]))
SELF = 15
NEAR_FIRST = tuple(range(15))


def offset_of(k):
    return [lax.shift_right_logical(jnp.int32(word), 2 * k) & 3 for word in PACKED]


def opposite(k):
    paired = ((k >= 1) & (k <= 4)) | ((k >= 7) & (k <= 14))
    return jnp.where(paired, k + 2 * lax.rem(k, 2) - 1, k)


def kernel(
    x_ref, g_ref, gain_ref, mask_ref, gate_hbm, up_hbm, down_hbm,
    outf_hbm, outb_hbm,
    wgu, wd, wgu_t, wd_t, xin, cin, recv_f, recv_b, send_f, send_b, hsend, csend,
    ret_f, ret_b, pre, rows, xg, dgu, gain_in, gain_out,
    load_sem, xin_sem, cin_sem, rsf_sem, rsb_sem, retf_sem, retb_sem, send_sem, out_sem,
):
    me = lax.axis_index("pipe")
    my = lax.axis_index("tensor")
    my_a, my_b = my // 4, lax.rem(my, 4)
    rows_of = xin.shape[1]
    width = xin.shape[2]
    hidden = wd.shape[0]
    blocks = hidden // BLOCK
    last = 7

    def to(k):
        a, b = OFFSETS[k]
        return lax.rem(my_a + a, 4) * 4 + lax.rem(my_b + b, 4)

    def source(k):
        a, b = OFFSETS[k]
        return lax.rem(my_a + (4 - a), 4) * 4 + lax.rem(my_b + (4 - b), 4)

    def cols(k):
        return pl.ds(k * CHUNK, CHUNK)

    def lanes(c):
        return pl.ds(pl.multiple_of(c * CHUNK, CHUNK), CHUNK)

    def remote(src, dst, sent, got, stage, index):
        return pltpu.make_async_remote_copy(
            src_ref=src, dst_ref=dst, send_sem=sent, recv_sem=got,
            device_id=(stage, index), device_id_type=MESH,
        )

    loads = []
    for k in range(16):
        rows_hbm = lanes(source(k))
        loads.append(pltpu.make_async_copy(
            gate_hbm.at[0, rows_hbm, :], wgu.at[pl.ds(k * CHUNK, CHUNK), pl.ds(0, hidden)], load_sem.at[0, k]))
        loads.append(pltpu.make_async_copy(
            up_hbm.at[0, rows_hbm, :], wgu.at[pl.ds(k * CHUNK, CHUNK), pl.ds(hidden, hidden)], load_sem.at[1, k]))
    for k in range(16):
        loads.append(pltpu.make_async_copy(
            down_hbm.at[0, :, lanes(to(k))], wd.at[:, cols(k)], load_sem.at[2, k]))
    for copy in loads:
        copy.start()

    barrier = pltpu.get_barrier_semaphore()
    for k in range(15):
        pl.semaphore_signal(barrier, inc=1, device_id=(me, to(k)), device_id_type=MESH)

    @pl.when(me > 0)
    def _():
        for k in range(16):
            pl.semaphore_signal(barrier, inc=1, device_id=(me - 1, to(k)), device_id_type=MESH)

    @pl.when(me < last)
    def _():
        for k in range(16):
            pl.semaphore_signal(barrier, inc=1, device_id=(me + 1, to(k)), device_id_type=MESH)

    for k in range(16):
        gain_in[:, k * CHUNK:(k + 1) * CHUNK] = gain_ref[:, lanes(source(k))]
        gain_out[:, k * CHUNK:(k + 1) * CHUNK] = gain_ref[:, lanes(to(k))]

    def keep(which, i, j):
        return jnp.full((BLOCK, BLOCK), mask_ref[0, which, i, j].astype(F32)).astype(BF16)

    @pl.loop(0, 16)
    def _(k):
        a, b = offset_of(k)
        c = lax.rem(my_a + 4 - a, 4) * 4 + lax.rem(my_b + 4 - b, 4)
        at = pl.ds(pl.multiple_of(k * CHUNK, CHUNK), CHUNK)
        for which in range(2):
            piece = wgu.at[at, pl.ds(which * hidden, hidden)]
            pltpu.make_async_copy(piece, piece, load_sem.at[which, k]).wait()
        for half in range(2):
            r = pl.ds(pl.multiple_of(k * CHUNK + half * BLOCK, BLOCK), BLOCK)
            for which in range(2):
                for j in range(blocks):
                    o = which * hidden + j * BLOCK
                    wgu[r, o:o + BLOCK] = wgu[r, o:o + BLOCK] * keep(which, c * 2 + half, j)

    edge = (me == 0) | (me == last)

    @pl.when(edge)
    def _():
        pl.semaphore_wait(barrier, 31)

    @pl.when(jnp.logical_not(edge))
    def _():
        pl.semaphore_wait(barrier, 47)

    def gather(src_ref, dst, got, sent):
        for m in range(MB):
            src = src_ref.at[pl.ds(m * rows_of, rows_of), :]
            pltpu.make_async_copy(src, dst.at[m, :, cols(SELF)], got.at[m, GROUP_OF[SELF]]).start()
            for k in NEAR_FIRST:
                remote(src, dst.at[m, :, cols(k)], sent.at[m], got.at[m, GROUP_OF[k]], me, to(k)).start()

    @pl.when(me == 0)
    def _():
        gather(x_ref, xin, xin_sem, send_sem.at[4])

    @pl.when(me == last)
    def _():
        gather(g_ref, cin, cin_sem, send_sem.at[4])

    @pl.loop(0, 16)
    def _(k):
        a, b = offset_of(k)
        c = lax.rem(my_a + a, 4) * 4 + lax.rem(my_b + b, 4)
        piece = wd.at[:, pl.ds(pl.multiple_of(k * CHUNK, CHUNK), CHUNK)]
        pltpu.make_async_copy(piece, piece, load_sem.at[2, k]).wait()
        for half in range(2):
            r = pl.ds(pl.multiple_of(k * CHUNK + half * BLOCK, BLOCK), BLOCK)
            for j in range(blocks):
                o = j * BLOCK
                wd[o:o + BLOCK, r] = wd[o:o + BLOCK, r] * keep(2, c * 2 + half, j)

    def transpose_weights():
        @pl.loop(0, 16)
        def _(k):
            n = opposite(k)
            here = pl.ds(pl.multiple_of(k * CHUNK, CHUNK), CHUNK)
            there = pl.ds(pl.multiple_of(n * CHUNK, CHUNK), CHUNK)
            for j in range(2 * hidden // CHUNK):
                o = j * CHUNK
                wgu_t[o:o + CHUNK, there] = wgu[here, o:o + CHUNK].T
            for j in range(blocks):
                o = j * BLOCK
                wd_t[there, o:o + BLOCK] = wd[o:o + BLOCK, here].T

    @pl.when(me >= 4)
    def _():
        transpose_weights()

    def whole(ref, sem):
        pltpu.make_async_copy(ref, ref, sem).wait()

    def arrived(ref, m, g, sem):
        lo, hi = GROUPS[g]
        span = slice(lo * CHUNK, hi * CHUNK)
        whole(ref.at[m, :, span], sem.at[m, g])
        return span

    def forward_compute(m):
        if FORWARD_AT < 0:
            @pl.when((m > 0) & (me < last))
            def _():
                forward_reduce(m - 1)

        square = jnp.zeros((rows_of, CHUNK), F32)
        for g, (lo, hi) in enumerate(GROUPS):
            span = arrived(xin, m, g, xin_sem)
            for k in range(lo, hi):
                one = slice(k * CHUNK, (k + 1) * CHUNK)
                part = xin[m, :, one].astype(F32)
                square = square + part * part
                xg[:, one] = (part * gain_in[:, one]).astype(BF16)
            part = jnp.dot(xg[:, span], wgu[span, :], preferred_element_type=F32)
            pre[m] = part if g == 0 else pre[m] + part

        @pl.when(me > 0)
        def _():
            remote(xin.at[m], ret_f.at[m], send_sem.at[5, m], retf_sem.at[m], me - 1, my).start()

        scale = lax.rsqrt(jnp.sum(square, axis=1, keepdims=True) * (1.0 / width) + EPS)
        rows[m] = jnp.broadcast_to(scale, (rows_of, BLOCK))
        both = pre[m] * scale
        pre[m] = both
        gate, up = both[:, :hidden], both[:, hidden:]
        act = (gate * jax.nn.sigmoid(gate) * up).astype(BF16)
        for n in range(4):
            o = n * 4 * CHUNK
            if n == FORWARD_AT:
                @pl.when((m > 0) & (me < last))
                def _():
                    forward_reduce(m - 1)

            part = jnp.dot(act, wd[:, o:o + 4 * CHUNK], preferred_element_type=F32)
            for q in range(4):
                send_f[m, n * 4 + q] = part[:, q * CHUNK:(q + 1) * CHUNK].astype(BF16)
            for q in range(4):
                k = n * 4 + q
                if k != SELF:
                    remote(send_f.at[m, k], recv_f.at[m, k], send_sem.at[0, m], rsf_sem.at[m], me, to(k)).start()

    def total(recv, send, m, sem):
        whole(recv.at[m, pl.ds(0, 15)], sem.at[m])
        acc = send[m, SELF].astype(F32)
        for k in range(15):
            acc = acc + recv[m, k].astype(F32)
        return acc

    own = slice(SELF * CHUNK, (SELF + 1) * CHUNK)

    def forward_reduce(m):
        acc = total(recv_f, send_f, m, rsf_sem)
        hsend[m] = (xin[m, :, own].astype(F32) + acc).astype(BF16)

        @pl.when(me < last)
        def _():
            for k in (*NEAR_FIRST, SELF):
                remote(hsend.at[m], xin.at[m, :, cols(k)], send_sem.at[1, m], xin_sem.at[m, GROUP_OF[k]], me + 1, to(k)).start()

        @pl.when(me == last)
        def _():
            ret_f[m, :, own] = hsend[m]
            for k in NEAR_FIRST:
                remote(hsend.at[m], ret_f.at[m, :, cols(k)], send_sem.at[1, m], retf_sem.at[m], me, to(k)).start()

    def backward_compute(m):
        if BACKWARD_AT < 0:
            @pl.when(m > 0)
            def _():
                backward_reduce(m - 1)

        dh = None
        for g in range(len(GROUPS)):
            span = arrived(cin, m, g, cin_sem)
            part = jnp.dot(cin[m, :, span], wd_t[span, :], preferred_element_type=F32)
            dh = part if dh is None else dh + part

        @pl.when(me < last)
        def _():
            remote(cin.at[m], ret_b.at[m], send_sem.at[6, m], retb_sem.at[m], me + 1, my).start()

        gate, up = pre[m, :, :hidden], pre[m, :, hidden:]
        sig = jax.nn.sigmoid(gate)
        dgate = (dh * up * sig * (1.0 + gate * (1.0 - sig))).astype(BF16)
        dup = (dh * gate * sig).astype(BF16)
        dgu[:, :hidden] = dgate
        dgu[:, hidden:] = dup
        inner = jnp.sum(dgate.astype(F32) * gate + dup.astype(F32) * up, axis=1, keepdims=True)
        scale = rows[m, :, 0:1]
        inner = inner * scale * scale * (1.0 / width)
        for n in range(4):
            o = n * 4 * CHUNK
            if n == BACKWARD_AT:
                @pl.when(m > 0)
                def _():
                    backward_reduce(m - 1)

            part = jnp.dot(dgu[...], wgu_t[:, o:o + 4 * CHUNK], preferred_element_type=F32)
            for q in range(4):
                k = n * 4 + q
                s = NEGATED[k]
                xval = xin[m, :, s * CHUNK:(s + 1) * CHUNK].astype(F32)
                back = part[:, q * CHUNK:(q + 1) * CHUNK] * gain_out[:, k * CHUNK:(k + 1) * CHUNK] * scale
                send_b[m, k] = (back - xval * inner).astype(BF16)
            for q in range(4):
                k = n * 4 + q
                if k != SELF:
                    remote(send_b.at[m, k], recv_b.at[m, k], send_sem.at[2, m], rsb_sem.at[m], me, to(k)).start()

    def backward_reduce(m):
        acc = total(recv_b, send_b, m, rsb_sem)
        csend[m] = (cin[m, :, own].astype(F32) + acc).astype(BF16)

        @pl.when(me > 0)
        def _():
            for k in (*NEAR_FIRST, SELF):
                remote(csend.at[m], cin.at[m, :, cols(k)], send_sem.at[3, m], cin_sem.at[m, GROUP_OF[k]], me - 1, to(k)).start()

        @pl.when(me == 0)
        def _():
            ret_b[m, :, own] = csend[m]
            for k in NEAR_FIRST:
                remote(csend.at[m], ret_b.at[m, :, cols(k)], send_sem.at[3, m], retb_sem.at[m], me, to(k)).start()

    turn = jnp.where(me == last, 0, MB + 1)

    @pl.loop(0, 2 * MB + 2)
    def _(i):
        back = i - turn

        @pl.when(i < MB)
        def _():
            forward_compute(i)

        @pl.when((i == MB) & (me < last))
        def _():
            forward_reduce(MB - 1)

        @pl.when((i == MB) & (me < 4))
        def _():
            transpose_weights()

        @pl.when((back >= 0) & (back < MB))
        def _():
            backward_compute(back)

        @pl.when(back == MB)
        def _():
            backward_reduce(MB - 1)

    @pl.when(me == last)
    def _():
        @pl.loop(0, MB)
        def _(m):
            forward_reduce(m)

    def put(ret, sem, out_hbm, which, edge):
        @pl.loop(0, MB)
        def _(m):
            @pl.when(me == edge)
            def _():
                whole(ret.at[m, :, pl.ds(0, 15 * CHUNK)], sem.at[m])

            @pl.when(me != edge)
            def _():
                whole(ret.at[m], sem.at[m])

            for k in range(16):
                pltpu.make_async_copy(
                    ret.at[m, :, cols(k)],
                    out_hbm.at[0, pl.ds(pl.multiple_of(m * rows_of, 16), rows_of), lanes(source(k))],
                    out_sem.at[which, m],
                ).start()

    put(ret_f, retf_sem, outf_hbm, 0, last)
    put(ret_b, retb_sem, outb_hbm, 1, 0)

    @pl.loop(0, MB)
    def _(m):
        fifteen = recv_f.at[m, pl.ds(0, 15)]
        whole(fifteen, send_sem.at[0, m])
        whole(fifteen, send_sem.at[2, m])

        @pl.when(me < last)
        def _():
            whole(xin.at[m], send_sem.at[1, m])
            whole(xin.at[m], send_sem.at[6, m])

        @pl.when(me == last)
        def _():
            whole(fifteen, send_sem.at[1, m])

        @pl.when(me > 0)
        def _():
            whole(xin.at[m], send_sem.at[3, m])
            whole(xin.at[m], send_sem.at[5, m])

        @pl.when(me == 0)
        def _():
            whole(fifteen, send_sem.at[3, m])

        @pl.when((me == 0) | (me == last))
        def _():
            whole(fifteen, send_sem.at[4, m])

        whole(ret_f.at[m], out_sem.at[0, m])
        whole(ret_b.at[m], out_sem.at[1, m])


def local(inputs, out_grad, norm_gain, gate_weight, up_weight, down_weight, block_mask):
    count, chunk = inputs.shape
    width = norm_gain.shape[1]
    hidden = gate_weight.shape[2]
    r = count // MB
    vmem = pl.BlockSpec(memory_space=pltpu.VMEM)
    anyspace = pl.BlockSpec(memory_space=pl.ANY)
    dma = pltpu.SemaphoreType.DMA
    full = lambda dtype=BF16: pltpu.VMEM((MB, r, width), dtype)
    parts = lambda: pltpu.VMEM((MB, 16, r, chunk), BF16)
    forward, backward = pl.pallas_call(
        kernel,
        out_shape=[jax.ShapeDtypeStruct((1, count, width), BF16)] * 2,
        in_specs=[vmem, vmem, vmem, pl.BlockSpec(memory_space=pltpu.SMEM), anyspace, anyspace, anyspace],
        out_specs=[anyspace, anyspace],
        scratch_shapes=[
            pltpu.VMEM((width, 2 * hidden), BF16),
            pltpu.VMEM((hidden, width), BF16),
            pltpu.VMEM((2 * hidden, width), BF16),
            pltpu.VMEM((width, hidden), BF16),
            full(), full(),
            parts(), parts(), parts(), parts(),
            pltpu.VMEM((MB, r, chunk), BF16),
            pltpu.VMEM((MB, r, chunk), BF16),
            full(), full(),
            pltpu.VMEM((MB, r, 2 * hidden), F32),
            pltpu.VMEM((MB, r, BLOCK), F32),
            pltpu.VMEM((r, width), BF16),
            pltpu.VMEM((r, 2 * hidden), BF16),
            pltpu.VMEM((1, width), F32),
            pltpu.VMEM((1, width), F32),
            dma((3, 16)),
            dma((MB, len(GROUPS))), dma((MB, len(GROUPS))), dma((MB,)), dma((MB,)), dma((MB,)), dma((MB,)),
            dma((7, MB)),
            dma((2, MB)),
        ],
        compiler_params=pltpu.CompilerParams(
            collective_id=0, has_side_effects=True, vmem_limit_bytes=67043328
        ),
        name="window",
    )(inputs, out_grad, norm_gain, block_mask, gate_weight, up_weight, down_weight)
    return forward.astype(F32), backward.astype(F32)


def solution(mesh):
    in_specs = (
        P(None, "tensor"),
        P(None, "tensor"),
        P("pipe", None),
        P("pipe", None, "tensor"),
        P("pipe", None, "tensor"),
        P("pipe", "tensor", None),
        P("pipe", None, None, "tensor"),
    )
    out_specs = (P("pipe", None, None), P("pipe", None, None))
    return jax.shard_map(local, mesh=mesh, in_specs=in_specs, out_specs=out_specs, check_vma=False)
```

```python
import functools

import jax
import jax.numpy as jnp
from jax import lax
from jax.experimental import pallas as pl
from jax.experimental.pallas import tpu as pltpu
from jax.sharding import PartitionSpec as P

EPS = 1e-05
MB = 4
PIECES = 4
CHUNK = 256
BLOCK = 128
F32 = jnp.float32
BF16 = jnp.bfloat16
MESH = pl.DeviceIdType.MESH

OFFSETS = [
    (2, 2),
    (2, 1), (2, 3), (1, 2), (3, 2),
    (2, 0), (0, 2), (1, 1), (3, 3), (1, 3), (3, 1),
    (1, 0), (3, 0), (0, 1), (0, 3),
    (0, 0),
]
NEGATED = [OFFSETS.index(((-a) % 4, (-b) % 4)) for a, b in OFFSETS]
GROUPS = ((11, 16), (5, 11), (0, 5))
FORWARD_AT = -1
BACKWARD_AT = -1
GROUP_OF = [next(g for g, (lo, hi) in enumerate(GROUPS) if lo <= k < hi) for k in range(16)]


def packed(values):
    word = sum(v << (2 * k) for k, v in enumerate(values))
    return word - (1 << 32) if word >= 1 << 31 else word


PACKED = (packed([a for a, b in OFFSETS]), packed([b for a, b in OFFSETS]))
SELF = 15
NEAR_FIRST = tuple(range(15))


def offset_of(k):
    return [lax.shift_right_logical(jnp.int32(word), 2 * k) & 3 for word in PACKED]


def opposite(k):
    paired = ((k >= 1) & (k <= 4)) | ((k >= 7) & (k <= 14))
    return jnp.where(paired, k + 2 * lax.rem(k, 2) - 1, k)


def kernel(
    x_ref, g_ref, gain_ref, mask_ref, gate_hbm, up_hbm, down_hbm,
    outf_hbm, outb_hbm,
    wgu, wd, wgu_t, wd_t, xin, cin, recv_f, recv_b, send_f, send_b, hsend, csend,
    ret_f, ret_b, pre, rows, xg, dgu, gain_in, gain_out,
    load_sem, xin_sem, cin_sem, rsf_sem, rsb_sem, retf_sem, retb_sem, send_sem, out_sem,
):
    me = lax.axis_index("pipe")
    my = lax.axis_index("tensor")
    my_a, my_b = my // 4, lax.rem(my, 4)
    rows_of = xin.shape[1]
    width = xin.shape[2]
    hidden = wd.shape[0]
    blocks = hidden // BLOCK
    last = 7

    def to(k):
        a, b = OFFSETS[k]
        return lax.rem(my_a + a, 4) * 4 + lax.rem(my_b + b, 4)

    def source(k):
        a, b = OFFSETS[k]
        return lax.rem(my_a + (4 - a), 4) * 4 + lax.rem(my_b + (4 - b), 4)

    def cols(k):
        return pl.ds(k * CHUNK, CHUNK)

    def lanes(c):
        return pl.ds(pl.multiple_of(c * CHUNK, CHUNK), CHUNK)

    def remote(src, dst, sent, got, stage, index):
        return pltpu.make_async_remote_copy(
            src_ref=src, dst_ref=dst, send_sem=sent, recv_sem=got,
            device_id=(stage, index), device_id_type=MESH,
        )

    loads = []
    for k in range(16):
        rows_hbm = lanes(source(k))
        loads.append(pltpu.make_async_copy(
            gate_hbm.at[0, rows_hbm, :], wgu.at[pl.ds(k * CHUNK, CHUNK), pl.ds(0, hidden)], load_sem.at[0, k]))
        loads.append(pltpu.make_async_copy(
            up_hbm.at[0, rows_hbm, :], wgu.at[pl.ds(k * CHUNK, CHUNK), pl.ds(hidden, hidden)], load_sem.at[1, k]))
    for k in range(16):
        loads.append(pltpu.make_async_copy(
            down_hbm.at[0, :, lanes(to(k))], wd.at[:, cols(k)], load_sem.at[2, k]))
    for copy in loads:
        copy.start()

    barrier = pltpu.get_barrier_semaphore()
    for k in range(15):
        pl.semaphore_signal(barrier, inc=1, device_id=(me, to(k)), device_id_type=MESH)

    @pl.when(me > 0)
    def _():
        for k in range(16):
            pl.semaphore_signal(barrier, inc=1, device_id=(me - 1, to(k)), device_id_type=MESH)

    @pl.when(me < last)
    def _():
        for k in range(16):
            pl.semaphore_signal(barrier, inc=1, device_id=(me + 1, to(k)), device_id_type=MESH)

    for k in range(16):
        gain_in[:, k * CHUNK:(k + 1) * CHUNK] = gain_ref[:, lanes(source(k))]
        gain_out[:, k * CHUNK:(k + 1) * CHUNK] = gain_ref[:, lanes(to(k))]

    def keep(which, i, j):
        return jnp.full((BLOCK, BLOCK), mask_ref[0, which, i, j].astype(F32)).astype(BF16)

    @pl.loop(0, 16)
    def _(k):
        a, b = offset_of(k)
        c = lax.rem(my_a + 4 - a, 4) * 4 + lax.rem(my_b + 4 - b, 4)
        at = pl.ds(pl.multiple_of(k * CHUNK, CHUNK), CHUNK)
        for which in range(2):
            piece = wgu.at[at, pl.ds(which * hidden, hidden)]
            pltpu.make_async_copy(piece, piece, load_sem.at[which, k]).wait()
        for half in range(2):
            r = pl.ds(pl.multiple_of(k * CHUNK + half * BLOCK, BLOCK), BLOCK)
            for which in range(2):
                for j in range(blocks):
                    o = which * hidden + j * BLOCK
                    wgu[r, o:o + BLOCK] = wgu[r, o:o + BLOCK] * keep(which, c * 2 + half, j)

    edge = (me == 0) | (me == last)

    @pl.when(edge)
    def _():
        pl.semaphore_wait(barrier, 31)

    @pl.when(jnp.logical_not(edge))
    def _():
        pl.semaphore_wait(barrier, 47)

    def gather(src_ref, dst, got, sent):
        for m in range(MB):
            src = src_ref.at[pl.ds(m * rows_of, rows_of), :]
            pltpu.make_async_copy(src, dst.at[m, :, cols(SELF)], got.at[m, GROUP_OF[SELF]]).start()
            for k in NEAR_FIRST:
                remote(src, dst.at[m, :, cols(k)], sent.at[m], got.at[m, GROUP_OF[k]], me, to(k)).start()

    @pl.when(me == 0)
    def _():
        gather(x_ref, xin, xin_sem, send_sem.at[4])

    @pl.when(me == last)
    def _():
        gather(g_ref, cin, cin_sem, send_sem.at[4])

    @pl.loop(0, 16)
    def _(k):
        a, b = offset_of(k)
        c = lax.rem(my_a + a, 4) * 4 + lax.rem(my_b + b, 4)
        piece = wd.at[:, pl.ds(pl.multiple_of(k * CHUNK, CHUNK), CHUNK)]
        pltpu.make_async_copy(piece, piece, load_sem.at[2, k]).wait()
        for half in range(2):
            r = pl.ds(pl.multiple_of(k * CHUNK + half * BLOCK, BLOCK), BLOCK)
            for j in range(blocks):
                o = j * BLOCK
                wd[o:o + BLOCK, r] = wd[o:o + BLOCK, r] * keep(2, c * 2 + half, j)

    def transpose_weights():
        @pl.loop(0, 16)
        def _(k):
            n = opposite(k)
            here = pl.ds(pl.multiple_of(k * CHUNK, CHUNK), CHUNK)
            there = pl.ds(pl.multiple_of(n * CHUNK, CHUNK), CHUNK)
            for j in range(2 * hidden // CHUNK):
                o = j * CHUNK
                wgu_t[o:o + CHUNK, there] = wgu[here, o:o + CHUNK].T
            for j in range(blocks):
                o = j * BLOCK
                wd_t[there, o:o + BLOCK] = wd[o:o + BLOCK, here].T

    @pl.when(me >= 4)
    def _():
        transpose_weights()

    def whole(ref, sem):
        pltpu.make_async_copy(ref, ref, sem).wait()

    def arrived(ref, m, g, sem):
        lo, hi = GROUPS[g]
        span = slice(lo * CHUNK, hi * CHUNK)
        whole(ref.at[m, :, span], sem.at[m, g])
        return span

    def forward_compute(m):
        if FORWARD_AT < 0:
            @pl.when((m > 0) & (me < last))
            def _():
                forward_reduce(m - 1)

        square = jnp.zeros((rows_of, CHUNK), F32)
        for g, (lo, hi) in enumerate(GROUPS):
            span = arrived(xin, m, g, xin_sem)
            for k in range(lo, hi):
                one = slice(k * CHUNK, (k + 1) * CHUNK)
                part = xin[m, :, one].astype(F32)
                square = square + part * part
                xg[:, one] = (part * gain_in[:, one]).astype(BF16)
            part = jnp.dot(xg[:, span], wgu[span, :], preferred_element_type=F32)
            pre[m] = part if g == 0 else pre[m] + part

        @pl.when(me > 0)
        def _():
            remote(xin.at[m], ret_f.at[m], send_sem.at[5, m], retf_sem.at[m], me - 1, my).start()

        scale = lax.rsqrt(jnp.sum(square, axis=1, keepdims=True) * (1.0 / width) + EPS)
        rows[m] = jnp.broadcast_to(scale, (rows_of, BLOCK))
        both = pre[m] * scale
        pre[m] = both
        gate, up = both[:, :hidden], both[:, hidden:]
        act = (gate * jax.nn.sigmoid(gate) * up).astype(BF16)
        for n in range(4):
            o = n * 4 * CHUNK
            if n == FORWARD_AT:
                @pl.when((m > 0) & (me < last))
                def _():
                    forward_reduce(m - 1)

            part = jnp.dot(act, wd[:, o:o + 4 * CHUNK], preferred_element_type=F32)
            for q in range(4):
                send_f[m, n * 4 + q] = part[:, q * CHUNK:(q + 1) * CHUNK].astype(BF16)
            for q in range(4):
                k = n * 4 + q
                if k != SELF:
                    remote(send_f.at[m, k], recv_f.at[m, k], send_sem.at[0, m], rsf_sem.at[m], me, to(k)).start()

    def total(recv, send, m, sem):
        whole(recv.at[m, pl.ds(0, 15)], sem.at[m])
        acc = send[m, SELF].astype(F32)
        for k in range(15):
            acc = acc + recv[m, k].astype(F32)
        return acc

    own = slice(SELF * CHUNK, (SELF + 1) * CHUNK)

    def forward_reduce(m):
        acc = total(recv_f, send_f, m, rsf_sem)
        hsend[m] = (xin[m, :, own].astype(F32) + acc).astype(BF16)

        @pl.when(me < last)
        def _():
            for k in (*NEAR_FIRST, SELF):
                remote(hsend.at[m], xin.at[m, :, cols(k)], send_sem.at[1, m], xin_sem.at[m, GROUP_OF[k]], me + 1, to(k)).start()

        @pl.when(me == last)
        def _():
            ret_f[m, :, own] = hsend[m]
            for k in NEAR_FIRST:
                remote(hsend.at[m], ret_f.at[m, :, cols(k)], send_sem.at[1, m], retf_sem.at[m], me, to(k)).start()

    def backward_compute(m):
        if BACKWARD_AT < 0:
            @pl.when((m > 0) & (m < MB - 1))
            def _():
                backward_reduce(m - 1)

        dh = None
        for g in range(len(GROUPS)):
            span = arrived(cin, m, g, cin_sem)
            part = jnp.dot(cin[m, :, span], wd_t[span, :], preferred_element_type=F32)
            dh = part if dh is None else dh + part

        @pl.when(me < last)
        def _():
            remote(cin.at[m], ret_b.at[m], send_sem.at[6, m], retb_sem.at[m], me + 1, my).start()

        gate, up = pre[m, :, :hidden], pre[m, :, hidden:]
        sig = jax.nn.sigmoid(gate)
        dgate = (dh * up * sig * (1.0 + gate * (1.0 - sig))).astype(BF16)
        dup = (dh * gate * sig).astype(BF16)
        dgu[:, :hidden] = dgate
        dgu[:, hidden:] = dup
        inner = jnp.sum(dgate.astype(F32) * gate + dup.astype(F32) * up, axis=1, keepdims=True)
        scale = rows[m, :, 0:1]
        inner = inner * scale * scale * (1.0 / width)
        for n in range(4):
            o = n * 4 * CHUNK
            if n == BACKWARD_AT:
                @pl.when(m > 0)
                def _():
                    backward_reduce(m - 1)

            part = jnp.dot(dgu[...], wgu_t[:, o:o + 4 * CHUNK], preferred_element_type=F32)
            for q in range(4):
                k = n * 4 + q
                s = NEGATED[k]
                xval = xin[m, :, s * CHUNK:(s + 1) * CHUNK].astype(F32)
                back = part[:, q * CHUNK:(q + 1) * CHUNK] * gain_out[:, k * CHUNK:(k + 1) * CHUNK] * scale
                send_b[m, k] = (back - xval * inner).astype(BF16)
            for q in range(4):
                k = n * 4 + q
                if k != SELF:
                    remote(send_b.at[m, k], recv_b.at[m, k], send_sem.at[2, m], rsb_sem.at[m], me, to(k)).start()

    def backward_reduce(m):
        acc = total(recv_b, send_b, m, rsb_sem)
        csend[m] = (cin[m, :, own].astype(F32) + acc).astype(BF16)

        @pl.when(me > 0)
        def _():
            for k in (*NEAR_FIRST, SELF):
                remote(csend.at[m], cin.at[m, :, cols(k)], send_sem.at[3, m], cin_sem.at[m, GROUP_OF[k]], me - 1, to(k)).start()

        @pl.when(me == 0)
        def _():
            ret_b[m, :, own] = csend[m]
            for k in NEAR_FIRST:
                remote(csend.at[m], ret_b.at[m, :, cols(k)], send_sem.at[3, m], retb_sem.at[m], me, to(k)).start()

    turn = jnp.where(me == last, 0, MB + 1)

    @pl.loop(0, 2 * MB + 2)
    def _(i):
        back = i - turn

        @pl.when(i < MB)
        def _():
            forward_compute(i)

        @pl.when((i == MB) & (me < last))
        def _():
            forward_reduce(MB - 1)

        @pl.when((i == MB) & (me < 4))
        def _():
            transpose_weights()

        @pl.when((back >= 0) & (back < MB))
        def _():
            backward_compute(back)

        @pl.when(back == MB)
        def _():
            for m in (MB - 2, MB - 1):
                backward_reduce(m)

    @pl.when(me == last)
    def _():
        @pl.loop(0, MB)
        def _(m):
            forward_reduce(m)

    def put(ret, sem, out_hbm, which, edge):
        @pl.loop(0, MB)
        def _(m):
            @pl.when(me == edge)
            def _():
                whole(ret.at[m, :, pl.ds(0, 15 * CHUNK)], sem.at[m])

            @pl.when(me != edge)
            def _():
                whole(ret.at[m], sem.at[m])

            for k in range(16):
                pltpu.make_async_copy(
                    ret.at[m, :, cols(k)],
                    out_hbm.at[0, pl.ds(pl.multiple_of(m * rows_of, 16), rows_of), lanes(source(k))],
                    out_sem.at[which, m],
                ).start()

    put(ret_f, retf_sem, outf_hbm, 0, last)
    put(ret_b, retb_sem, outb_hbm, 1, 0)

    @pl.loop(0, MB)
    def _(m):
        fifteen = recv_f.at[m, pl.ds(0, 15)]
        whole(fifteen, send_sem.at[0, m])
        whole(fifteen, send_sem.at[2, m])

        @pl.when(me < last)
        def _():
            whole(xin.at[m], send_sem.at[1, m])
            whole(xin.at[m], send_sem.at[6, m])

        @pl.when(me == last)
        def _():
            whole(fifteen, send_sem.at[1, m])

        @pl.when(me > 0)
        def _():
            whole(xin.at[m], send_sem.at[3, m])
            whole(xin.at[m], send_sem.at[5, m])

        @pl.when(me == 0)
        def _():
            whole(fifteen, send_sem.at[3, m])

        @pl.when((me == 0) | (me == last))
        def _():
            whole(fifteen, send_sem.at[4, m])

        whole(ret_f.at[m], out_sem.at[0, m])
        whole(ret_b.at[m], out_sem.at[1, m])


def widen(f_hbm, b_hbm, fo_hbm, bo_hbm, narrow, wide, got, put):
    r = narrow.shape[1] // PIECES
    order = [(a, p) for p in range(PIECES) for a in range(2)]
    src, dst = (f_hbm, b_hbm), (fo_hbm, bo_hbm)
    rows = lambda p: pl.ds(p * r, r)
    ins = [pltpu.make_async_copy(src[a].at[0, rows(p), :], narrow.at[a, rows(p), :], got.at[a, p]) for a, p in order]
    outs = [pltpu.make_async_copy(wide.at[a, rows(p), :], dst[a].at[0, rows(p), :], put.at[a, p]) for a, p in order]
    for copy in ins:
        copy.start()
    for (a, p), came, leaves in zip(order, ins, outs):
        came.wait()
        wide[a, p * r:(p + 1) * r, :] = narrow[a, p * r:(p + 1) * r, :].astype(F32)
        leaves.start()
    for copy in outs:
        copy.wait()


def local(inputs, out_grad, norm_gain, gate_weight, up_weight, down_weight, block_mask):
    count, chunk = inputs.shape
    width = norm_gain.shape[1]
    hidden = gate_weight.shape[2]
    r = count // MB
    vmem = pl.BlockSpec(memory_space=pltpu.VMEM)
    anyspace = pl.BlockSpec(memory_space=pl.ANY)
    dma = pltpu.SemaphoreType.DMA
    full = lambda dtype=BF16: pltpu.VMEM((MB, r, width), dtype)
    parts = lambda: pltpu.VMEM((MB, 16, r, chunk), BF16)
    forward, backward = pl.pallas_call(
        kernel,
        out_shape=[jax.ShapeDtypeStruct((1, count, width), BF16)] * 2,
        in_specs=[vmem, vmem, vmem, pl.BlockSpec(memory_space=pltpu.SMEM), anyspace, anyspace, anyspace],
        out_specs=[anyspace, anyspace],
        scratch_shapes=[
            pltpu.VMEM((width, 2 * hidden), BF16),
            pltpu.VMEM((hidden, width), BF16),
            pltpu.VMEM((2 * hidden, width), BF16),
            pltpu.VMEM((width, hidden), BF16),
            full(), full(),
            parts(), parts(), parts(), parts(),
            pltpu.VMEM((MB, r, chunk), BF16),
            pltpu.VMEM((MB, r, chunk), BF16),
            full(), full(),
            pltpu.VMEM((MB, r, 2 * hidden), F32),
            pltpu.VMEM((MB, r, BLOCK), F32),
            pltpu.VMEM((r, width), BF16),
            pltpu.VMEM((r, 2 * hidden), BF16),
            pltpu.VMEM((1, width), F32),
            pltpu.VMEM((1, width), F32),
            dma((3, 16)),
            dma((MB, len(GROUPS))), dma((MB, len(GROUPS))), dma((MB,)), dma((MB,)), dma((MB,)), dma((MB,)),
            dma((7, MB)),
            dma((2, MB)),
        ],
        compiler_params=pltpu.CompilerParams(
            collective_id=0, has_side_effects=True, vmem_limit_bytes=67043328
        ),
        name="window",
    )(inputs, out_grad, norm_gain, block_mask, gate_weight, up_weight, down_weight)
    return pl.pallas_call(
        widen,
        out_shape=[jax.ShapeDtypeStruct((1, count, width), F32)] * 2,
        in_specs=[anyspace] * 2,
        out_specs=[anyspace] * 2,
        scratch_shapes=[
            pltpu.VMEM((2, count, width), BF16),
            pltpu.VMEM((2, count, width), F32),
            dma((2, PIECES)), dma((2, PIECES)),
        ],
        compiler_params=pltpu.CompilerParams(vmem_limit_bytes=16 * 1024 * 1024),
        name="widen",
    )(forward, backward)


def solution(mesh):
    in_specs = (
        P(None, "tensor"),
        P(None, "tensor"),
        P("pipe", None),
        P("pipe", None, "tensor"),
        P("pipe", None, "tensor"),
        P("pipe", "tensor", None),
        P("pipe", None, None, "tensor"),
    )
    out_specs = (P("pipe", None, None), P("pipe", None, None))
    return jax.shard_map(local, mesh=mesh, in_specs=in_specs, out_specs=out_specs, check_vma=False)
```

```python
import functools

import jax
import jax.numpy as jnp
from jax import lax
from jax.experimental import pallas as pl
from jax.experimental.pallas import tpu as pltpu
from jax.sharding import PartitionSpec as P

EPS = 1e-05
MB = 4
PIECES = 4
CHUNK = 256
BLOCK = 128
F32 = jnp.float32
BF16 = jnp.bfloat16
MESH = pl.DeviceIdType.MESH

OFFSETS = [
    (2, 2),
    (2, 1), (2, 3), (1, 2), (3, 2),
    (2, 0), (0, 2), (1, 1), (3, 3), (1, 3), (3, 1),
    (1, 0), (3, 0), (0, 1), (0, 3),
    (0, 0),
]
NEGATED = [OFFSETS.index(((-a) % 4, (-b) % 4)) for a, b in OFFSETS]
GROUPS = ((11, 16), (5, 11), (0, 5))
FORWARD_AT = -1
BACKWARD_AT = -1
GROUP_OF = [next(g for g, (lo, hi) in enumerate(GROUPS) if lo <= k < hi) for k in range(16)]


def packed(values):
    word = sum(v << (2 * k) for k, v in enumerate(values))
    return word - (1 << 32) if word >= 1 << 31 else word


PACKED = (packed([a for a, b in OFFSETS]), packed([b for a, b in OFFSETS]))
SELF = 15
SEND_ORDER = (0, 6, 3, 4, 13, 14, 1, 2, 7, 8, 9, 10, 5, 11, 12)


def offset_of(k):
    return [lax.shift_right_logical(jnp.int32(word), 2 * k) & 3 for word in PACKED]


def opposite(k):
    paired = ((k >= 1) & (k <= 4)) | ((k >= 7) & (k <= 14))
    return jnp.where(paired, k + 2 * lax.rem(k, 2) - 1, k)


def kernel(
    x_ref, g_ref, gain_ref, mask_ref, gate_hbm, up_hbm, down_hbm,
    outf_hbm, outb_hbm,
    wgu, wd, wgu_t, wd_t, xin, cin, recv_f, recv_b, send_f, send_b, hsend, csend,
    ret_f, ret_b, pre, rows, xg, dgu, gain_in, gain_out,
    load_sem, xin_sem, cin_sem, rsf_sem, rsb_sem, retf_sem, retb_sem, send_sem, out_sem,
):
    me = lax.axis_index("pipe")
    my = lax.axis_index("tensor")
    my_a, my_b = my // 4, lax.rem(my, 4)
    rows_of = xin.shape[1]
    width = xin.shape[2]
    hidden = wd.shape[0]
    blocks = hidden // BLOCK
    last = 7

    def to(k):
        a, b = OFFSETS[k]
        return lax.rem(my_a + a, 4) * 4 + lax.rem(my_b + b, 4)

    def source(k):
        a, b = OFFSETS[k]
        return lax.rem(my_a + (4 - a), 4) * 4 + lax.rem(my_b + (4 - b), 4)

    def cols(k):
        return pl.ds(k * CHUNK, CHUNK)

    def lanes(c):
        return pl.ds(pl.multiple_of(c * CHUNK, CHUNK), CHUNK)

    def remote(src, dst, sent, got, stage, index):
        return pltpu.make_async_remote_copy(
            src_ref=src, dst_ref=dst, send_sem=sent, recv_sem=got,
            device_id=(stage, index), device_id_type=MESH,
        )

    loads = []
    for k in range(16):
        rows_hbm = lanes(source(k))
        loads.append(pltpu.make_async_copy(
            gate_hbm.at[0, rows_hbm, :], wgu.at[pl.ds(k * CHUNK, CHUNK), pl.ds(0, hidden)], load_sem.at[0, k]))
        loads.append(pltpu.make_async_copy(
            up_hbm.at[0, rows_hbm, :], wgu.at[pl.ds(k * CHUNK, CHUNK), pl.ds(hidden, hidden)], load_sem.at[1, k]))
    for k in range(16):
        loads.append(pltpu.make_async_copy(
            down_hbm.at[0, :, lanes(to(k))], wd.at[:, cols(k)], load_sem.at[2, k]))
    for copy in loads:
        copy.start()

    barrier = pltpu.get_barrier_semaphore()
    for k in range(15):
        pl.semaphore_signal(barrier, inc=1, device_id=(me, to(k)), device_id_type=MESH)

    @pl.when(me > 0)
    def _():
        for k in range(16):
            pl.semaphore_signal(barrier, inc=1, device_id=(me - 1, to(k)), device_id_type=MESH)

    @pl.when(me < last)
    def _():
        for k in range(16):
            pl.semaphore_signal(barrier, inc=1, device_id=(me + 1, to(k)), device_id_type=MESH)

    for k in range(16):
        gain_in[:, k * CHUNK:(k + 1) * CHUNK] = gain_ref[:, lanes(source(k))]
        gain_out[:, k * CHUNK:(k + 1) * CHUNK] = gain_ref[:, lanes(to(k))]

    def keep(which, i, j):
        return jnp.full((BLOCK, BLOCK), mask_ref[0, which, i, j].astype(F32)).astype(BF16)

    @pl.loop(0, 16)
    def _(k):
        a, b = offset_of(k)
        c = lax.rem(my_a + 4 - a, 4) * 4 + lax.rem(my_b + 4 - b, 4)
        at = pl.ds(pl.multiple_of(k * CHUNK, CHUNK), CHUNK)
        for which in range(2):
            piece = wgu.at[at, pl.ds(which * hidden, hidden)]
            pltpu.make_async_copy(piece, piece, load_sem.at[which, k]).wait()
        for half in range(2):
            r = pl.ds(pl.multiple_of(k * CHUNK + half * BLOCK, BLOCK), BLOCK)
            for which in range(2):
                for j in range(blocks):
                    o = which * hidden + j * BLOCK
                    wgu[r, o:o + BLOCK] = wgu[r, o:o + BLOCK] * keep(which, c * 2 + half, j)

    edge = (me == 0) | (me == last)

    @pl.when(edge)
    def _():
        pl.semaphore_wait(barrier, 31)

    @pl.when(jnp.logical_not(edge))
    def _():
        pl.semaphore_wait(barrier, 47)

    def gather(src_ref, dst, got, sent):
        for m in range(MB):
            src = src_ref.at[pl.ds(m * rows_of, rows_of), :]
            pltpu.make_async_copy(src, dst.at[m, :, cols(SELF)], got.at[m, GROUP_OF[SELF]]).start()
            for k in SEND_ORDER:
                remote(src, dst.at[m, :, cols(k)], sent.at[m], got.at[m, GROUP_OF[k]], me, to(k)).start()

    @pl.when(me == 0)
    def _():
        gather(x_ref, xin, xin_sem, send_sem.at[4])

    @pl.when(me == last)
    def _():
        gather(g_ref, cin, cin_sem, send_sem.at[4])

    @pl.loop(0, 16)
    def _(k):
        a, b = offset_of(k)
        c = lax.rem(my_a + a, 4) * 4 + lax.rem(my_b + b, 4)
        piece = wd.at[:, pl.ds(pl.multiple_of(k * CHUNK, CHUNK), CHUNK)]
        pltpu.make_async_copy(piece, piece, load_sem.at[2, k]).wait()
        for half in range(2):
            r = pl.ds(pl.multiple_of(k * CHUNK + half * BLOCK, BLOCK), BLOCK)
            for j in range(blocks):
                o = j * BLOCK
                wd[o:o + BLOCK, r] = wd[o:o + BLOCK, r] * keep(2, c * 2 + half, j)

    def transpose_weights():
        @pl.loop(0, 16)
        def _(k):
            n = opposite(k)
            here = pl.ds(pl.multiple_of(k * CHUNK, CHUNK), CHUNK)
            there = pl.ds(pl.multiple_of(n * CHUNK, CHUNK), CHUNK)
            for j in range(2 * hidden // CHUNK):
                o = j * CHUNK
                wgu_t[o:o + CHUNK, there] = wgu[here, o:o + CHUNK].T
            for j in range(blocks):
                o = j * BLOCK
                wd_t[there, o:o + BLOCK] = wd[o:o + BLOCK, here].T

    @pl.when(me >= 4)
    def _():
        transpose_weights()

    def whole(ref, sem):
        pltpu.make_async_copy(ref, ref, sem).wait()

    def arrived(ref, m, g, sem):
        lo, hi = GROUPS[g]
        span = slice(lo * CHUNK, hi * CHUNK)
        whole(ref.at[m, :, span], sem.at[m, g])
        return span

    def forward_compute(m):
        if FORWARD_AT < 0:
            @pl.when((m > 0) & (me < last))
            def _():
                forward_reduce(m - 1)

        square = jnp.zeros((rows_of, CHUNK), F32)
        for g, (lo, hi) in enumerate(GROUPS):
            span = arrived(xin, m, g, xin_sem)
            for k in range(lo, hi):
                one = slice(k * CHUNK, (k + 1) * CHUNK)
                part = xin[m, :, one].astype(F32)
                square = square + part * part
                xg[:, one] = (part * gain_in[:, one]).astype(BF16)
            part = jnp.dot(xg[:, span], wgu[span, :], preferred_element_type=F32)
            pre[m] = part if g == 0 else pre[m] + part

        @pl.when(me > 0)
        def _():
            remote(xin.at[m], ret_f.at[m], send_sem.at[5, m], retf_sem.at[m], me - 1, my).start()

        scale = lax.rsqrt(jnp.sum(square, axis=1, keepdims=True) * (1.0 / width) + EPS)
        rows[m] = jnp.broadcast_to(scale, (rows_of, BLOCK))
        both = pre[m] * scale
        pre[m] = both
        gate, up = both[:, :hidden], both[:, hidden:]
        act = (gate * jax.nn.sigmoid(gate) * up).astype(BF16)
        for n in range(4):
            o = n * 4 * CHUNK
            if n == FORWARD_AT:
                @pl.when((m > 0) & (me < last))
                def _():
                    forward_reduce(m - 1)

            part = jnp.dot(act, wd[:, o:o + 4 * CHUNK], preferred_element_type=F32)
            for q in range(4):
                send_f[m, n * 4 + q] = part[:, q * CHUNK:(q + 1) * CHUNK].astype(BF16)
            for q in range(4):
                k = n * 4 + q
                if k != SELF:
                    remote(send_f.at[m, k], recv_f.at[m, k], send_sem.at[0, m], rsf_sem.at[m], me, to(k)).start()

    def total(recv, send, m, sem):
        whole(recv.at[m, pl.ds(0, 15)], sem.at[m])
        acc = send[m, SELF].astype(F32)
        for k in range(15):
            acc = acc + recv[m, k].astype(F32)
        return acc

    own = slice(SELF * CHUNK, (SELF + 1) * CHUNK)

    def forward_reduce(m):
        acc = total(recv_f, send_f, m, rsf_sem)
        hsend[m] = (xin[m, :, own].astype(F32) + acc).astype(BF16)

        @pl.when(me < last)
        def _():
            for k in (*SEND_ORDER, SELF):
                remote(hsend.at[m], xin.at[m, :, cols(k)], send_sem.at[1, m], xin_sem.at[m, GROUP_OF[k]], me + 1, to(k)).start()

        @pl.when(me == last)
        def _():
            ret_f[m, :, own] = hsend[m]
            for k in SEND_ORDER:
                remote(hsend.at[m], ret_f.at[m, :, cols(k)], send_sem.at[1, m], retf_sem.at[m], me, to(k)).start()

    def backward_compute(m):
        if BACKWARD_AT < 0:
            @pl.when((m > 0) & (m < MB - 1))
            def _():
                backward_reduce(m - 1)

        dh = None
        for g in range(len(GROUPS)):
            span = arrived(cin, m, g, cin_sem)
            part = jnp.dot(cin[m, :, span], wd_t[span, :], preferred_element_type=F32)
            dh = part if dh is None else dh + part

        @pl.when(me < last)
        def _():
            remote(cin.at[m], ret_b.at[m], send_sem.at[6, m], retb_sem.at[m], me + 1, my).start()

        gate, up = pre[m, :, :hidden], pre[m, :, hidden:]
        sig = jax.nn.sigmoid(gate)
        dgate = (dh * up * sig * (1.0 + gate * (1.0 - sig))).astype(BF16)
        dup = (dh * gate * sig).astype(BF16)
        dgu[:, :hidden] = dgate
        dgu[:, hidden:] = dup
        inner = jnp.sum(dgate.astype(F32) * gate + dup.astype(F32) * up, axis=1, keepdims=True)
        scale = rows[m, :, 0:1]
        inner = inner * scale * scale * (1.0 / width)
        for n in range(4):
            o = n * 4 * CHUNK
            if n == BACKWARD_AT:
                @pl.when(m > 0)
                def _():
                    backward_reduce(m - 1)

            part = jnp.dot(dgu[...], wgu_t[:, o:o + 4 * CHUNK], preferred_element_type=F32)
            for q in range(4):
                k = n * 4 + q
                s = NEGATED[k]
                xval = xin[m, :, s * CHUNK:(s + 1) * CHUNK].astype(F32)
                back = part[:, q * CHUNK:(q + 1) * CHUNK] * gain_out[:, k * CHUNK:(k + 1) * CHUNK] * scale
                send_b[m, k] = (back - xval * inner).astype(BF16)
            for q in range(4):
                k = n * 4 + q
                if k != SELF:
                    remote(send_b.at[m, k], recv_b.at[m, k], send_sem.at[2, m], rsb_sem.at[m], me, to(k)).start()

    def backward_reduce(m):
        acc = total(recv_b, send_b, m, rsb_sem)
        csend[m] = (cin[m, :, own].astype(F32) + acc).astype(BF16)

        @pl.when(me > 0)
        def _():
            for k in (*SEND_ORDER, SELF):
                remote(csend.at[m], cin.at[m, :, cols(k)], send_sem.at[3, m], cin_sem.at[m, GROUP_OF[k]], me - 1, to(k)).start()

        @pl.when(me == 0)
        def _():
            ret_b[m, :, own] = csend[m]
            for k in SEND_ORDER:
                remote(csend.at[m], ret_b.at[m, :, cols(k)], send_sem.at[3, m], retb_sem.at[m], me, to(k)).start()

    turn = jnp.where(me == last, 0, MB + 1)

    @pl.loop(0, 2 * MB + 2)
    def _(i):
        back = i - turn

        @pl.when(i < MB)
        def _():
            forward_compute(i)

        @pl.when((i == MB) & (me < last))
        def _():
            forward_reduce(MB - 1)

        @pl.when((i == MB) & (me < 4))
        def _():
            transpose_weights()

        @pl.when((back >= 0) & (back < MB))
        def _():
            backward_compute(back)

        @pl.when(back == MB)
        def _():
            for m in (MB - 2, MB - 1):
                backward_reduce(m)

    @pl.when(me == last)
    def _():
        @pl.loop(0, MB)
        def _(m):
            forward_reduce(m)

    def put(ret, sem, out_hbm, which, edge):
        @pl.loop(0, MB)
        def _(m):
            @pl.when(me == edge)
            def _():
                whole(ret.at[m, :, pl.ds(0, 15 * CHUNK)], sem.at[m])

            @pl.when(me != edge)
            def _():
                whole(ret.at[m], sem.at[m])

            for k in range(16):
                pltpu.make_async_copy(
                    ret.at[m, :, cols(k)],
                    out_hbm.at[0, pl.ds(pl.multiple_of(m * rows_of, 16), rows_of), lanes(source(k))],
                    out_sem.at[which, m],
                ).start()

    put(ret_f, retf_sem, outf_hbm, 0, last)
    put(ret_b, retb_sem, outb_hbm, 1, 0)

    @pl.loop(0, MB)
    def _(m):
        fifteen = recv_f.at[m, pl.ds(0, 15)]
        whole(fifteen, send_sem.at[0, m])
        whole(fifteen, send_sem.at[2, m])

        @pl.when(me < last)
        def _():
            whole(xin.at[m], send_sem.at[1, m])
            whole(xin.at[m], send_sem.at[6, m])

        @pl.when(me == last)
        def _():
            whole(fifteen, send_sem.at[1, m])

        @pl.when(me > 0)
        def _():
            whole(xin.at[m], send_sem.at[3, m])
            whole(xin.at[m], send_sem.at[5, m])

        @pl.when(me == 0)
        def _():
            whole(fifteen, send_sem.at[3, m])

        @pl.when((me == 0) | (me == last))
        def _():
            whole(fifteen, send_sem.at[4, m])

        whole(ret_f.at[m], out_sem.at[0, m])
        whole(ret_b.at[m], out_sem.at[1, m])


def widen(f_hbm, b_hbm, fo_hbm, bo_hbm, narrow, wide, got, put):
    r = narrow.shape[1] // PIECES
    order = [(a, p) for p in range(PIECES) for a in range(2)]
    src, dst = (f_hbm, b_hbm), (fo_hbm, bo_hbm)
    rows = lambda p: pl.ds(p * r, r)
    ins = [pltpu.make_async_copy(src[a].at[0, rows(p), :], narrow.at[a, rows(p), :], got.at[a, p]) for a, p in order]
    outs = [pltpu.make_async_copy(wide.at[a, rows(p), :], dst[a].at[0, rows(p), :], put.at[a, p]) for a, p in order]
    for copy in ins:
        copy.start()
    for (a, p), came, leaves in zip(order, ins, outs):
        came.wait()
        wide[a, p * r:(p + 1) * r, :] = narrow[a, p * r:(p + 1) * r, :].astype(F32)
        leaves.start()
    for copy in outs:
        copy.wait()


def local(inputs, out_grad, norm_gain, gate_weight, up_weight, down_weight, block_mask):
    count, chunk = inputs.shape
    width = norm_gain.shape[1]
    hidden = gate_weight.shape[2]
    r = count // MB
    vmem = pl.BlockSpec(memory_space=pltpu.VMEM)
    anyspace = pl.BlockSpec(memory_space=pl.ANY)
    dma = pltpu.SemaphoreType.DMA
    full = lambda dtype=BF16: pltpu.VMEM((MB, r, width), dtype)
    parts = lambda: pltpu.VMEM((MB, 16, r, chunk), BF16)
    forward, backward = pl.pallas_call(
        kernel,
        out_shape=[jax.ShapeDtypeStruct((1, count, width), BF16)] * 2,
        in_specs=[vmem, vmem, vmem, pl.BlockSpec(memory_space=pltpu.SMEM), anyspace, anyspace, anyspace],
        out_specs=[anyspace, anyspace],
        scratch_shapes=[
            pltpu.VMEM((width, 2 * hidden), BF16),
            pltpu.VMEM((hidden, width), BF16),
            pltpu.VMEM((2 * hidden, width), BF16),
            pltpu.VMEM((width, hidden), BF16),
            full(), full(),
            parts(), parts(), parts(), parts(),
            pltpu.VMEM((MB, r, chunk), BF16),
            pltpu.VMEM((MB, r, chunk), BF16),
            full(), full(),
            pltpu.VMEM((MB, r, 2 * hidden), F32),
            pltpu.VMEM((MB, r, BLOCK), F32),
            pltpu.VMEM((r, width), BF16),
            pltpu.VMEM((r, 2 * hidden), BF16),
            pltpu.VMEM((1, width), F32),
            pltpu.VMEM((1, width), F32),
            dma((3, 16)),
            dma((MB, len(GROUPS))), dma((MB, len(GROUPS))), dma((MB,)), dma((MB,)), dma((MB,)), dma((MB,)),
            dma((7, MB)),
            dma((2, MB)),
        ],
        compiler_params=pltpu.CompilerParams(
            collective_id=0, has_side_effects=True, vmem_limit_bytes=67043328
        ),
        name="window",
    )(inputs, out_grad, norm_gain, block_mask, gate_weight, up_weight, down_weight)
    return pl.pallas_call(
        widen,
        out_shape=[jax.ShapeDtypeStruct((1, count, width), F32)] * 2,
        in_specs=[anyspace] * 2,
        out_specs=[anyspace] * 2,
        scratch_shapes=[
            pltpu.VMEM((2, count, width), BF16),
            pltpu.VMEM((2, count, width), F32),
            dma((2, PIECES)), dma((2, PIECES)),
        ],
        compiler_params=pltpu.CompilerParams(vmem_limit_bytes=16 * 1024 * 1024),
        name="widen",
    )(forward, backward)


def solution(mesh):
    in_specs = (
        P(None, "tensor"),
        P(None, "tensor"),
        P("pipe", None),
        P("pipe", None, "tensor"),
        P("pipe", None, "tensor"),
        P("pipe", "tensor", None),
        P("pipe", None, None, "tensor"),
    )
    out_specs = (P("pipe", None, None), P("pipe", None, None))
    return jax.shard_map(local, mesh=mesh, in_specs=in_specs, out_specs=out_specs, check_vma=False)
```
